128 devices in a mesh: oi: 4 (over z_lo, core), oj: 4 (over y), vir: 8 (over z_hi, x).
Axes of the slice: x: 4, y: 4, z: 4 (z_hi: 2, z_lo: 2; z = z_hi * 2 + z_lo), core: 2. Of those that a mesh axis runs over, the one named last changes fastest.
Arguments:
- amplitudes: float32 [8, 8, 1024, 1024], P('oi', 'oj', 'vir'), may hold values from -6 to 6
- integrals: float32 [8, 8, 1024, 1024], P('oi', 'oj', 'vir'), may hold values from -0.0007324219 to 0.0007324219
- fock_virtual: float32 [1024, 1024], P('vir'), may hold values from -0.1875 to 0.1875
- screening: int32 [4, 4, 8, 8], P('oi', 'oj'), may hold values 0 or 1
Outputs:
- symmetric_residual: float32 [8, 8, 1024, 1024], P('oi', 'oj', 'vir')
The draws below stay inside these ranges and needn't reach their ends.
Inputs may be any that keep to these rules, and one draw needn't show every extreme that they name: `screening`: entry (p, q, s, t) screens virtual blocks s and t of occupied block pair p, q.
All inputs are finite; a program needn't handle non-finite values.
Results may differ from the reference program's by a relative error of at most 0.00007.
Values sent between devices are 32-bit elements; how exact they have to be, the bound alone decides.
A program may use at most 128 MiB of HBM per device.

```python
import jax
import jax.numpy as jnp
from jax import lax

OCC_DEV = 2
V = 1024
BLK = 128
NOCC = 8
VB = 8
N_OI = 4
N_OJ = 4


def plant(values, key, low, largest):
    longest = values.shape.index(max(values.shape))
    spots = []
    for shift in (0, 1):
        where = [jax.random.randint(jax.random.fold_in(key, axis), (), 0, length) for axis, length in enumerate(values.shape)]
        where[longest] = (where[longest] + shift) % values.shape[longest]
        spots.append(tuple(where))
    return values.at[spots[0]].set(low).at[spots[1]].set(largest)


def block_scale(stream_key, dims, split, smallest, largest):
    gain = 1.0
    for dim, blocks in split:
        heights = jax.random.uniform(jax.random.fold_in(jax.random.fold_in(stream_key, 6), dim), (blocks,), jnp.float32, smallest / len(split), largest / len(split))
        gain = gain * jnp.repeat(jnp.exp(heights), dims[dim] // blocks).reshape((-1,) + (1,) * (len(dims) - 1 - dim))
    return gain


def gaussian(key, extent, scale, bound, split=(), kind=jnp.bfloat16):
    result = jax.random.normal(key, extent, jnp.float32) * scale
    if len(split) > 0:
        result = block_scale(key, extent, split, -0.22, 0.18) * result
    return jnp.clip(result, min=-bound, max=bound).astype(kind)


def setup_inputs(seed: int = 0) -> dict:
    key_list = jax.random.split(jax.random.key(seed), 5)
    amplitudes = gaussian(key_list[0], (NOCC, NOCC, V, V), 1.0, 6.0, ((0, 4), (1, 4), (2, 8)), jnp.float32)
    integrals = gaussian(key_list[1], (NOCC, NOCC, V, V), (NOCC * NOCC * V * V) ** -0.5, 0.0007324219, ((0, 4), (1, 4), (2, 8)), jnp.float32)
    fock_virtual = gaussian(key_list[2], (V, V), V ** -0.5, 0.1875, ((0, 8),), jnp.float32)
    screening = plant((jax.random.randint(key_list[3], (N_OI, N_OJ, VB, VB), 0, 3) < 2).astype(jnp.int32), jax.random.fold_in(key_list[3], 1), 0, 1)
    return dict(amplitudes=amplitudes, integrals=integrals, fock_virtual=fock_virtual, screening=screening)


def reference(amplitudes, integrals, fock_virtual, screening):
    kept = jnp.repeat(jnp.repeat(screening, OCC_DEV, axis=0), OCC_DEV, axis=1)
    kept = jnp.repeat(jnp.repeat(kept, BLK, axis=2), BLK, axis=3).astype(jnp.float32)
    screened = amplitudes * kept
    pair_sum = jnp.einsum("ijad,ijcd->ac", screened, integrals, precision=lax.Precision.HIGHEST)
    dressed = fock_virtual - pair_sum
    cycle = jnp.einsum("ac,ijcb->ijab", dressed, screened, precision=lax.Precision.HIGHEST)
    cycle = cycle + jnp.einsum("ijac,bc->ijab", screened, dressed, precision=lax.Precision.HIGHEST)
    return cycle + jnp.transpose(cycle, (1, 0, 3, 2))
```

```python
import jax
import jax.numpy as jnp
from jax import lax
from jax.sharding import PartitionSpec as P

BLK = 128
high = lax.Precision.HIGH


def mirror_perm(n):
    return [(a * n + b, b * n + a) for a in range(n) for b in range(n)]


def turn(values, n):
    swapped = jnp.transpose(values, (1, 0, 2, 3))
    sent = lax.all_to_all(swapped, "vir", split_axis=3, concat_axis=2, tiled=True)
    return lax.ppermute(sent, ("oi", "oj"), mirror_perm(n))


def body(amplitudes, integrals, fock_virtual, screening):
    occ = amplitudes.shape[0]
    rows_here = amplitudes.shape[2]
    width = amplitudes.shape[3]
    pairs = occ * occ
    n = lax.axis_size("oi")
    vir_place = lax.axis_index("vir")
    nblocks = rows_here // BLK
    block_rows = lax.dynamic_slice(
        screening[0, 0], (vir_place * nblocks, jnp.int32(0)), (nblocks, width // BLK)
    )
    dense = jnp.repeat(jnp.repeat(block_rows.astype(jnp.float32), BLK, axis=0), BLK, axis=1)
    screened = amplitudes * dense[None, None]
    turned = turn(screened, n)
    turned_integrals = turn(integrals, n)
    partial = jnp.einsum("ijad,ijcd->ac", turned, turned_integrals, precision=high)
    share = lax.psum_scatter(partial, ("vir", "oi", "oj"), scatter_dimension=0, tiled=True)
    place = lax.axis_index("oi") * n + lax.axis_index("oj")
    mine = lax.dynamic_slice_in_dim(fock_virtual, place * share.shape[0], share.shape[0], 0)
    dressed = lax.all_gather(mine - share, ("vir", "oi", "oj"), axis=0, tiled=True)
    both = screened + jnp.transpose(turned, (0, 1, 3, 2))
    half = jnp.einsum("pac,bc->pab", both.reshape(pairs, rows_here, width), dressed, precision=high)
    half = half.reshape(occ, occ, rows_here, width)
    return half + jnp.transpose(turn(half, n), (0, 1, 3, 2))


def solution(mesh):
    placed = (
        P("oi", "oj", "vir", None),
        P("oi", "oj", "vir", None),
        P("vir", None),
        P("oi", "oj", None, None),
    )
    return jax.shard_map(
        body, mesh=mesh, in_specs=placed, out_specs=P("oi", "oj", "vir", None), check_vma=False
    )
```

```python
import functools

import jax
import jax.numpy as jnp
from jax import lax
from jax.experimental import pallas as pl
from jax.experimental.pallas import tpu as pltpu
from jax.sharding import PartitionSpec as P

BLK = 128
MESH = pl.DeviceIdType.MESH
high = lax.Precision.HIGH
COLORS = ((0, 384), (384, 384), (768, 256))


def places():
    return lax.axis_index("oi"), lax.axis_index("oj"), lax.axis_index("vir")


def ring_places(v):
    half, x = v // 4, v % 4
    order = ((1, 2), (0, 2), (1, 1), (1, 3), (0, 1), (0, 3), (1, 0), (0, 0))
    return [((half + dh) % 2) * 4 + (x + dx) % 4 for dh, dx in order]


def turn_kernel(count, *refs):
    sources, targets = refs[:count], refs[count : 2 * count]
    send_sem, recv_sem, own_sem = refs[2 * count :]
    oi, oj, v = places()
    others = ring_places(v)
    apart = jnp.where(oi == oj, 0, 1)
    barrier = pltpu.get_barrier_semaphore()
    for w in others[:-1]:
        pl.semaphore_signal(barrier, inc=1, device_id=(oj, oi, w), device_id_type=MESH)

    @pl.when(oi != oj)
    def _():
        pl.semaphore_signal(barrier, inc=1, device_id=(oj, oi, v), device_id_type=MESH)

    pl.semaphore_wait(barrier, 7 + apart)

    def remote(k, w, frm):
        return pltpu.make_async_remote_copy(
            src_ref=sources[k].at[:, :, pl.ds(pl.multiple_of(w * BLK, BLK), BLK)],
            dst_ref=targets[k].at[:, pl.ds(pl.multiple_of(frm * BLK, BLK), BLK), :],
            send_sem=send_sem.at[k, w],
            recv_sem=recv_sem.at[k, frm],
            device_id=(oj, oi, w),
            device_id_type=MESH,
        )

    def own(k):
        return pltpu.make_async_copy(
            sources[k].at[:, :, pl.ds(pl.multiple_of(v * BLK, BLK), BLK)],
            targets[k].at[:, pl.ds(pl.multiple_of(v * BLK, BLK), BLK), :],
            own_sem.at[k],
        )

    for k in range(count):
        for w in others[:-1]:
            remote(k, w, v).start()

        @pl.when(oi != oj)
        def _():
            remote(k, v, v).start()

        @pl.when(oi == oj)
        def _():
            own(k).start()

    for k in range(count):
        for w in others[:-1]:
            remote(k, w, w).wait_recv()
            remote(k, w, v).wait_send()

        @pl.when(oi != oj)
        def _():
            remote(k, v, v).wait()

        @pl.when(oi == oj)
        def _():
            own(k).wait()


def turn(cid, *arrays):
    count = len(arrays)
    pairs, rows, width = arrays[0].shape
    vmem = pl.BlockSpec(memory_space=pltpu.VMEM)
    return pl.pallas_call(
        functools.partial(turn_kernel, count),
        out_shape=[jax.ShapeDtypeStruct((pairs, width, rows), jnp.float32)] * count,
        in_specs=[vmem] * count,
        out_specs=[vmem] * count,
        scratch_shapes=[
            pltpu.SemaphoreType.DMA((count, 8)),
            pltpu.SemaphoreType.DMA((count, 8)),
            pltpu.SemaphoreType.DMA((count,)),
        ],
        compiler_params=pltpu.CompilerParams(collective_id=cid, has_side_effects=True),
        name=f"turn{count}",
    )(*arrays)


def gray_bits(p):
    return ((p + 1) // 2) % 2, p // 2


def dressing_kernel(p_ref, fock_ref, d_ref, acc, got, core_got, rs_send, rs_recv, ag_send, ag_recv):
    oi, oj, v = places()
    core, low = oi % 2, oi // 2
    half, x = v // 4, v % 4
    z = half * 2 + low
    bits = [gray_bits(x), gray_bits(oj), gray_bits(z)]
    first = [
        (oi, oj, half * 4 + x + 1 - 2 * (x % 2)),
        (oi, oj + 1 - 2 * (oj % 2), v),
        ((oi + 2) % 4, oj, v),
    ]
    second = [
        (oi, oj, half * 4 + 3 - x),
        (oi, 3 - oj, v),
        ((oi + 2) % 4, oj, (v + 4) % 8),
    ]
    twin = (oi + 1 - 2 * core, oj, v)

    barrier = pltpu.get_barrier_semaphore()
    for peer in [twin] + first + second:
        pl.semaphore_signal(barrier, inc=1, device_id=peer, device_id_type=MESH)
    pl.semaphore_wait(barrier, 7)

    def step(g, k):
        j = (g + k) % 6
        axis = j % 3
        letter = (j // 3 + core) % 2
        peer = tuple(a + letter * (b - a) for a, b in zip(first[axis], second[axis]))
        bit = bits[axis][0] + letter * (bits[axis][1] - bits[axis][0])
        return peer, bit

    def rows(start, size):
        return pl.ds(pl.multiple_of(start, 8), size)

    def core_copy(g):
        c0, cn = COLORS[g]
        return pltpu.make_async_remote_copy(
            src_ref=p_ref.at[rows((1 - core) * 512, 512), pl.ds(c0, cn)],
            dst_ref=core_got.at[:, pl.ds(c0, cn)],
            send_sem=rs_send.at[0, g],
            recv_sem=rs_recv.at[0, g],
            device_id=twin,
            device_id_type=MESH,
        )

    def rs_copy(g, k, start):
        c0, cn = COLORS[g]
        size = 256 >> k
        peer, bit = step(g, k)
        return pltpu.make_async_remote_copy(
            src_ref=acc.at[rows(start + (1 - bit) * size, size), pl.ds(c0, cn)],
            dst_ref=got.at[pl.ds(size, size), pl.ds(c0, cn)],
            send_sem=rs_send.at[k + 1, g],
            recv_sem=rs_recv.at[k + 1, g],
            device_id=peer,
            device_id_type=MESH,
        )

    def ag_copy(g, k, start, place):
        c0, cn = COLORS[g]
        size = 256 >> k
        peer, _ = step(g, k)
        here = d_ref.at[rows(core * 512 + start + place * size, size), pl.ds(c0, cn)]
        return pltpu.make_async_remote_copy(
            src_ref=here,
            dst_ref=here,
            send_sem=ag_send.at[k + 1, g],
            recv_sem=ag_recv.at[k + 1, g],
            device_id=peer,
            device_id_type=MESH,
        )

    def core_back(g, which):
        c0, cn = COLORS[g]
        here = d_ref.at[rows(which * 512, 512), pl.ds(c0, cn)]
        return pltpu.make_async_remote_copy(
            src_ref=here,
            dst_ref=here,
            send_sem=ag_send.at[0, g],
            recv_sem=ag_recv.at[0, g],
            device_id=twin,
            device_id_type=MESH,
        )

    colours = range(3)
    for g in colours:
        core_copy(g).start()
    starts = [[jnp.int32(0)] for _ in colours]
    for g in colours:
        c0, cn = COLORS[g]
        core_copy(g).wait_recv()
        acc[:, pl.ds(c0, cn)] = p_ref[rows(core * 512, 512), pl.ds(c0, cn)] + core_got[:, pl.ds(c0, cn)]

        @pl.when((oj == 0) & (oi == half))
        def _():
            acc[rows(x * BLK, BLK), pl.ds(c0, cn)] -= fock_ref[:, pl.ds(c0, cn)]

        rs_copy(g, 0, starts[g][0]).start()
    for k in range(6):
        size = 256 >> k
        for g in colours:
            c0, cn = COLORS[g]
            _, bit = step(g, k)
            rs_copy(g, k, starts[g][k]).wait_recv()
            mine = starts[g][k] + bit * size
            starts[g].append(mine)
            total = acc[rows(mine, size), pl.ds(c0, cn)] + got[pl.ds(size, size), pl.ds(c0, cn)]
            if k < 5:
                acc[rows(mine, size), pl.ds(c0, cn)] = total
                rs_copy(g, k + 1, mine).start()
            else:
                d_ref[rows(core * 512 + mine, size), pl.ds(c0, cn)] = -total
                _, bit = step(g, 5)
                ag_copy(g, 5, starts[g][5], bit).start()
    for k in range(5, -1, -1):
        for g in colours:
            _, bit = step(g, k)
            ag_copy(g, k, starts[g][k], 1 - bit).wait_recv()
            if k > 0:
                _, bit = step(g, k - 1)
                ag_copy(g, k - 1, starts[g][k - 1], bit).start()
            else:
                core_back(g, core).start()
    for g in colours:
        core_back(g, 1 - core).wait_recv()
    for g in colours:
        core_copy(g).wait_send()
        core_back(g, core).wait_send()
        for k in range(6):
            _, bit = step(g, k)
            rs_copy(g, k, starts[g][k]).wait_send()
            ag_copy(g, k, starts[g][k], bit).wait_send()


def dressing(partial, fock):
    vmem = pl.BlockSpec(memory_space=pltpu.VMEM)
    size = partial.shape[0]
    return pl.pallas_call(
        dressing_kernel,
        out_shape=jax.ShapeDtypeStruct((size, size), jnp.float32),
        in_specs=[vmem] * 2,
        out_specs=vmem,
        scratch_shapes=[
            pltpu.VMEM((512, 1024), jnp.float32),
            pltpu.VMEM((512, 1024), jnp.float32),
            pltpu.VMEM((512, 1024), jnp.float32),
            pltpu.SemaphoreType.DMA((7, 3)),
            pltpu.SemaphoreType.DMA((7, 3)),
            pltpu.SemaphoreType.DMA((7, 3)),
            pltpu.SemaphoreType.DMA((7, 3)),
        ],
        compiler_params=pltpu.CompilerParams(collective_id=1, has_side_effects=True),
        name="dressing",
    )(partial, fock)


def body(amplitudes, integrals, fock_virtual, screening):
    occ = amplitudes.shape[0]
    rows_here = amplitudes.shape[2]
    width = amplitudes.shape[3]
    pairs = occ * occ
    vir_place = lax.axis_index("vir")
    block_rows = lax.dynamic_slice(screening[0, 0], (vir_place, jnp.int32(0)), (1, width // BLK))
    dense = jnp.repeat(block_rows.astype(jnp.float32), BLK, axis=1)
    screened = amplitudes.reshape(pairs, rows_here, width) * dense[None]
    turned, turned_integrals = turn(2, screened, integrals.reshape(pairs, rows_here, width))
    partial = jnp.einsum("pad,pcd->ac", turned, turned_integrals, precision=high)
    dressed = dressing(partial, fock_virtual)

    def mirrored(values):
        values = values.reshape(occ, occ, width, rows_here)
        return jnp.transpose(values, (1, 0, 3, 2)).reshape(pairs, rows_here, width)

    both = screened + mirrored(turned)
    term = jnp.einsum("pac,bc->pab", both, dressed, precision=high)
    (back,) = turn(3, term)
    out = term + mirrored(back)
    return out.reshape(occ, occ, rows_here, width)


def solution(mesh):
    placed = (
        P("oi", "oj", "vir", None),
        P("oi", "oj", "vir", None),
        P("vir", None),
        P("oi", "oj", None, None),
    )
    return jax.shard_map(
        body, mesh=mesh, in_specs=placed, out_specs=P("oi", "oj", "vir", None), check_vma=False
    )
```

```python
import functools

import jax
import jax.numpy as jnp
from jax import lax
from jax.experimental import pallas as pl
from jax.experimental.pallas import tpu as pltpu
from jax.sharding import PartitionSpec as P

BLK = 128
MESH = pl.DeviceIdType.MESH
high = lax.Precision.HIGH
COLORS = ((0, 384), (384, 384), (768, 256))


def places():
    return lax.axis_index("oi"), lax.axis_index("oj"), lax.axis_index("vir")


ORDER = ((1, 2), (0, 2), (1, 1), (1, 3), (0, 1), (0, 3), (1, 0), (0, 0))
PARTS = 2


def ring_place(v, dh, dx):
    return ((v // 4 + dh % 2) % 2) * 4 + (v % 4 + dx % 4) % 4


class Turn:
    def __init__(self, sources, targets, holds, sems):
        self.sources, self.targets, self.holds = sources, targets, holds
        self.send, self.recv, self.hold_recv, self.forward_send, self.own_sem = sems
        self.oi, self.oj, self.v = places()
        self.same = self.oi == self.oj
        self.apart = (self.oi + 2) % 4 == self.oj
        self.cross = self.oi + self.oj == 3
        self.plain = jnp.logical_not(self.same | self.apart)

    def greet(self):
        oi, oj, v = self.oi, self.oj, self.v
        barrier = pltpu.get_barrier_semaphore()

        def signal(a, b, w):
            pl.semaphore_signal(barrier, inc=1, device_id=(a, b, w), device_id_type=MESH)

        def everyone(a, b, itself):
            for dh, dx in ORDER if itself else ORDER[:-1]:
                signal(a, b, ring_place(v, dh, dx))

        @pl.when(self.same)
        def _():
            everyone(oi, oi, False)
            everyone((oi + 2) % 4, oi, True)
            signal(oi, 3 - oi, v)

        @pl.when(self.apart)
        def _():
            everyone(oj, oj, True)
            signal(oi, 3 - oi, v)

        @pl.when(self.plain)
        def _():
            everyone(oj, oi, True)

            @pl.when(self.cross)
            def _():
                signal(oi, oi, v)
                signal(oi, (oi + 2) % 4, v)

        pl.semaphore_wait(
            barrier,
            jnp.where(self.same, 16, jnp.where(self.apart, 9, jnp.where(self.cross, 10, 8))),
        )

    def tile(self, k, w, part):
        pairs = self.sources[k].shape[0] // PARTS
        return self.sources[k].at[pl.ds(part * pairs, pairs), :, pl.ds(pl.multiple_of(w * BLK, BLK), BLK)]

    def slot(self, array, frm, part):
        pairs = array.shape[0] // PARTS
        return array.at[pl.ds(part * pairs, pairs), pl.ds(pl.multiple_of(frm * BLK, BLK), BLK), :]

    def straight(self, k, w, frm, part):
        return pltpu.make_async_remote_copy(
            src_ref=self.tile(k, w, part),
            dst_ref=self.slot(self.targets[k], frm, part),
            send_sem=self.send.at[k, w, part],
            recv_sem=self.recv.at[k, frm, part],
            device_id=(self.oj, self.oi, w),
            device_id_type=MESH,
        )

    def detour(self, k, w, part):
        return pltpu.make_async_remote_copy(
            src_ref=self.tile(k, w, part),
            dst_ref=self.slot(self.holds[k], self.v, part),
            send_sem=self.send.at[k, w, part],
            recv_sem=self.hold_recv.at[k, self.v, part],
            device_id=(self.oj, self.oj, w),
            device_id_type=MESH,
        )

    def forward(self, k, frm, part, last):
        return pltpu.make_async_remote_copy(
            src_ref=self.slot(self.holds[k], frm, part),
            dst_ref=self.slot((self.targets if last else self.holds)[k], frm, part),
            send_sem=self.forward_send.at[k, frm, part],
            recv_sem=(self.recv if last else self.hold_recv).at[k, frm, part],
            device_id=(self.oi, (self.oi + 2) % 4 if last else 3 - self.oi, self.v),
            device_id_type=MESH,
        )

    def own(self, k):
        return pltpu.make_async_copy(
            self.sources[k].at[:, :, pl.ds(pl.multiple_of(self.v * BLK, BLK), BLK)],
            self.targets[k].at[:, pl.ds(pl.multiple_of(self.v * BLK, BLK), BLK), :],
            self.own_sem.at[k],
        )

    def start(self, k):
        @pl.when(self.apart)
        def _():
            for dh, dx in ORDER:
                for part in range(PARTS):
                    self.detour(k, ring_place(self.v, dh, dx), part).start()

        @pl.when(self.plain)
        def _():
            for dh, dx in ORDER:
                for part in range(PARTS):
                    self.straight(k, ring_place(self.v, dh, dx), self.v, part).start()

        @pl.when(self.same)
        def _():
            for dh, dx in ORDER[:-1]:
                for part in range(PARTS):
                    self.straight(k, ring_place(self.v, dh, dx), self.v, part).start()
            self.own(k).start()

    def relay(self, k, j):
        dh, dx = ORDER[j]
        frm = ring_place(self.v, -dh, -dx)
        for part in range(PARTS):

            @pl.when(self.same)
            def _():
                self.forward(k, frm, part, False).wait_recv()
                self.forward(k, frm, part, False).start()

            @pl.when(self.cross)
            def _():
                self.forward(k, frm, part, False).wait_recv()
                self.forward(k, frm, part, True).start()

    def arrive(self, k, j):
        dh, dx = ORDER[j]
        frm = ring_place(self.v, -dh, -dx)

        def wait():
            for part in range(PARTS):
                self.straight(k, frm, frm, part).wait_recv()

        if j < len(ORDER) - 1:
            wait()
        else:
            pl.when(self.same)(lambda: self.own(k).wait())
            pl.when(jnp.logical_not(self.same))(wait)

    def drain(self, k):
        for j, (dh, dx) in enumerate(ORDER):
            w = ring_place(self.v, dh, dx)
            for part in range(PARTS):
                if j < len(ORDER) - 1:
                    self.straight(k, w, w, part).wait_send()
                else:

                    @pl.when(jnp.logical_not(self.same))
                    def _():
                        self.straight(k, w, w, part).wait_send()

                @pl.when(self.same | self.cross)
                def _():
                    self.forward(k, w, part, True).wait_send()


def turn_sems(count):
    shape = (count, 8, PARTS)
    return [pltpu.SemaphoreType.DMA(shape)] * 4 + [pltpu.SemaphoreType.DMA((count,))]


def turn_kernel(count, *refs):
    sources, targets, holds = refs[:count], refs[count : 2 * count], refs[2 * count : 3 * count]
    moves = Turn(sources, targets, holds, refs[3 * count :])
    moves.greet()
    for k in range(count):
        moves.start(k)
    for k in range(count):
        for j in range(8):
            moves.relay(k, j)
    for k in range(count):
        for j in range(8):
            moves.arrive(k, j)
        moves.drain(k)


def turn(cid, *arrays):
    count = len(arrays)
    pairs, rows, width = arrays[0].shape
    vmem = pl.BlockSpec(memory_space=pltpu.VMEM)
    return pl.pallas_call(
        functools.partial(turn_kernel, count),
        out_shape=[jax.ShapeDtypeStruct((pairs, width, rows), jnp.float32)] * count,
        in_specs=[vmem] * count,
        out_specs=[vmem] * count,
        scratch_shapes=[pltpu.VMEM((pairs, width, rows), jnp.float32)] * count + turn_sems(count),
        compiler_params=pltpu.CompilerParams(collective_id=cid, has_side_effects=True),
        name=f"turn{count}",
    )(*arrays)


def gray_bits(p):
    return ((p + 1) // 2) % 2, p // 2


def dressing_kernel(p_ref, fock_ref, d_ref, acc, got, core_got, rs_send, rs_recv, ag_send, ag_recv):
    oi, oj, v = places()
    core, low = oi % 2, oi // 2
    half, x = v // 4, v % 4
    z = half * 2 + low
    bits = [gray_bits(x), gray_bits(oj), gray_bits(z)]
    first = [
        (oi, oj, half * 4 + x + 1 - 2 * (x % 2)),
        (oi, oj + 1 - 2 * (oj % 2), v),
        ((oi + 2) % 4, oj, v),
    ]
    second = [
        (oi, oj, half * 4 + 3 - x),
        (oi, 3 - oj, v),
        ((oi + 2) % 4, oj, (v + 4) % 8),
    ]
    twin = (oi + 1 - 2 * core, oj, v)

    barrier = pltpu.get_barrier_semaphore()
    for peer in [twin] + first + second:
        pl.semaphore_signal(barrier, inc=1, device_id=peer, device_id_type=MESH)
    pl.semaphore_wait(barrier, 7)

    def step(g, k):
        j = (g + k) % 6
        axis = j % 3
        letter = (j // 3 + core) % 2
        peer = tuple(a + letter * (b - a) for a, b in zip(first[axis], second[axis]))
        bit = bits[axis][0] + letter * (bits[axis][1] - bits[axis][0])
        return peer, bit

    def rows(start, size):
        return pl.ds(pl.multiple_of(start, 8), size)

    def core_copy(g):
        c0, cn = COLORS[g]
        return pltpu.make_async_remote_copy(
            src_ref=p_ref.at[rows((1 - core) * 512, 512), pl.ds(c0, cn)],
            dst_ref=core_got.at[:, pl.ds(c0, cn)],
            send_sem=rs_send.at[0, g],
            recv_sem=rs_recv.at[0, g],
            device_id=twin,
            device_id_type=MESH,
        )

    def rs_copy(g, k, start):
        c0, cn = COLORS[g]
        size = 256 >> k
        peer, bit = step(g, k)
        return pltpu.make_async_remote_copy(
            src_ref=acc.at[rows(start + (1 - bit) * size, size), pl.ds(c0, cn)],
            dst_ref=got.at[pl.ds(size, size), pl.ds(c0, cn)],
            send_sem=rs_send.at[k + 1, g],
            recv_sem=rs_recv.at[k + 1, g],
            device_id=peer,
            device_id_type=MESH,
        )

    def ag_copy(g, k, start, place):
        c0, cn = COLORS[g]
        size = 256 >> k
        peer, _ = step(g, k)
        here = d_ref.at[rows(core * 512 + start + place * size, size), pl.ds(c0, cn)]
        return pltpu.make_async_remote_copy(
            src_ref=here,
            dst_ref=here,
            send_sem=ag_send.at[k + 1, g],
            recv_sem=ag_recv.at[k + 1, g],
            device_id=peer,
            device_id_type=MESH,
        )

    def core_back(g, which):
        c0, cn = COLORS[g]
        here = d_ref.at[rows(which * 512, 512), pl.ds(c0, cn)]
        return pltpu.make_async_remote_copy(
            src_ref=here,
            dst_ref=here,
            send_sem=ag_send.at[0, g],
            recv_sem=ag_recv.at[0, g],
            device_id=twin,
            device_id_type=MESH,
        )

    colours = range(3)
    for g in colours:
        core_copy(g).start()
    starts = [[jnp.int32(0)] for _ in colours]
    for g in colours:
        c0, cn = COLORS[g]
        core_copy(g).wait_recv()
        acc[:, pl.ds(c0, cn)] = p_ref[rows(core * 512, 512), pl.ds(c0, cn)] + core_got[:, pl.ds(c0, cn)]

        @pl.when((oj == 0) & (oi == half))
        def _():
            acc[rows(x * BLK, BLK), pl.ds(c0, cn)] -= fock_ref[:, pl.ds(c0, cn)]

        rs_copy(g, 0, starts[g][0]).start()
    for k in range(6):
        size = 256 >> k
        for g in colours:
            c0, cn = COLORS[g]
            _, bit = step(g, k)
            rs_copy(g, k, starts[g][k]).wait_recv()
            mine = starts[g][k] + bit * size
            starts[g].append(mine)
            total = acc[rows(mine, size), pl.ds(c0, cn)] + got[pl.ds(size, size), pl.ds(c0, cn)]
            if k < 5:
                acc[rows(mine, size), pl.ds(c0, cn)] = total
                rs_copy(g, k + 1, mine).start()
            else:
                d_ref[rows(core * 512 + mine, size), pl.ds(c0, cn)] = -total
                _, bit = step(g, 5)
                ag_copy(g, 5, starts[g][5], bit).start()
    for k in range(5, -1, -1):
        for g in colours:
            _, bit = step(g, k)
            ag_copy(g, k, starts[g][k], 1 - bit).wait_recv()
            if k > 0:
                _, bit = step(g, k - 1)
                ag_copy(g, k - 1, starts[g][k - 1], bit).start()
            else:
                core_back(g, core).start()
    for g in colours:
        core_back(g, 1 - core).wait_recv()
    for g in colours:
        core_copy(g).wait_send()
        core_back(g, core).wait_send()
        for k in range(6):
            _, bit = step(g, k)
            rs_copy(g, k, starts[g][k]).wait_send()
            ag_copy(g, k, starts[g][k], bit).wait_send()


def dressing(partial, fock):
    vmem = pl.BlockSpec(memory_space=pltpu.VMEM)
    size = partial.shape[0]
    return pl.pallas_call(
        dressing_kernel,
        out_shape=jax.ShapeDtypeStruct((size, size), jnp.float32),
        in_specs=[vmem] * 2,
        out_specs=vmem,
        scratch_shapes=[
            pltpu.VMEM((512, 1024), jnp.float32),
            pltpu.VMEM((512, 1024), jnp.float32),
            pltpu.VMEM((512, 1024), jnp.float32),
            pltpu.SemaphoreType.DMA((7, 3)),
            pltpu.SemaphoreType.DMA((7, 3)),
            pltpu.SemaphoreType.DMA((7, 3)),
            pltpu.SemaphoreType.DMA((7, 3)),
        ],
        compiler_params=pltpu.CompilerParams(collective_id=1, has_side_effects=True),
        name="dressing",
    )(partial, fock)


def body(amplitudes, integrals, fock_virtual, screening):
    occ = amplitudes.shape[0]
    rows_here = amplitudes.shape[2]
    width = amplitudes.shape[3]
    pairs = occ * occ
    vir_place = lax.axis_index("vir")
    block_rows = lax.dynamic_slice(screening[0, 0], (vir_place, jnp.int32(0)), (1, width // BLK))
    dense = jnp.repeat(block_rows.astype(jnp.float32), BLK, axis=1)
    screened = amplitudes.reshape(pairs, rows_here, width) * dense[None]
    turned, turned_integrals = turn(2, screened, integrals.reshape(pairs, rows_here, width))
    partial = jnp.einsum("pad,pcd->ac", turned, turned_integrals, precision=high)
    dressed = dressing(partial, fock_virtual)

    def mirrored(values):
        values = values.reshape(occ, occ, width, rows_here)
        return jnp.transpose(values, (1, 0, 3, 2)).reshape(pairs, rows_here, width)

    both = screened + mirrored(turned)
    term = jnp.einsum("pac,bc->pab", both, dressed, precision=high)
    (back,) = turn(3, term)
    out = term + mirrored(back)
    return out.reshape(occ, occ, rows_here, width)


def solution(mesh):
    placed = (
        P("oi", "oj", "vir", None),
        P("oi", "oj", "vir", None),
        P("vir", None),
        P("oi", "oj", None, None),
    )
    return jax.shard_map(
        body, mesh=mesh, in_specs=placed, out_specs=P("oi", "oj", "vir", None), check_vma=False
    )
```

```python
import functools

import jax
import jax.numpy as jnp
from jax import lax
from jax.experimental import pallas as pl
from jax.experimental.pallas import tpu as pltpu
from jax.sharding import PartitionSpec as P

BLK = 128
MESH = pl.DeviceIdType.MESH
COLORS = ((0, 384), (384, 384), (768, 256))
ORDER = ((0, 2), (1, 2), (0, 1), (0, 3), (1, 1), (1, 3), (1, 0), (0, 0))
RELAYED = 4
PARTS = 2
NT = (((1,), (1,)), ((), ()))


def places():
    return lax.axis_index("oi"), lax.axis_index("oj"), lax.axis_index("vir")


def ring_place(v, dh, dx):
    return ((v // 4 + dh % 2) % 2) * 4 + (v % 4 + dx % 4) % 4


def block(w):
    return pl.ds(pl.multiple_of(w * BLK, BLK), BLK)


def rows8(start, size):
    return pl.ds(pl.multiple_of(start, 8), size)


def split(values):
    top = values.astype(jnp.bfloat16)
    return top, (values - top.astype(jnp.float32)).astype(jnp.bfloat16)


def product(a, b):
    (a1, a2), (b1, b2) = a, b
    dot = functools.partial(lax.dot_general, dimension_numbers=NT, preferred_element_type=jnp.float32)
    return dot(a1, b1) + (dot(a1, b2) + dot(a2, b1))


def remote(source, target, send, recv, peer):
    return pltpu.make_async_remote_copy(
        src_ref=source, dst_ref=target, send_sem=send, recv_sem=recv, device_id=peer, device_id_type=MESH
    )


class Turn:
    def __init__(self, sources, targets, holds, sems):
        self.sources, self.targets, self.holds = sources, targets, holds
        self.send, self.recv, self.hold_recv, self.forward_send, self.own_sem = sems
        self.oi, self.oj, self.v = places()
        self.same = self.oi == self.oj
        self.apart = (self.oi + 2) % 4 == self.oj
        self.cross = self.oi + self.oj == 3

    def greet(self, more):
        oi, oj, v = self.oi, self.oj, self.v
        barrier = pltpu.get_barrier_semaphore()

        def signal(*peers):
            for peer in peers:
                pl.semaphore_signal(barrier, inc=1, device_id=peer, device_id_type=MESH)

        def everyone(a, b):
            return [(a, b, ring_place(v, dh, dx)) for dh, dx in ORDER]

        signal(*more, *everyone(oj, oi)[:-1])

        @pl.when(jnp.logical_not(self.same))
        def _():
            signal((oj, oi, v))

        @pl.when(self.same)
        def _():
            signal(*everyone((oi + 2) % 4, oi), (oi, 3 - oi, v))

        @pl.when(self.apart)
        def _():
            signal(*everyone(oj, oj), (oi, 3 - oi, v))

        @pl.when(self.cross)
        def _():
            signal((oi, oi, v), (oi, (oi + 2) % 4, v))

        kinds = jnp.where(self.same, 16, jnp.where(self.apart, 17, jnp.where(self.cross, 10, 8)))
        pl.semaphore_wait(barrier, kinds + len(more))

    def tile(self, k, w, part):
        pairs = self.sources[k].shape[0] // PARTS
        return self.sources[k].at[pl.ds(part * pairs, pairs), :, block(w)]

    def slot(self, array, frm, part):
        pairs = array.shape[0] // PARTS
        return array.at[pl.ds(part * pairs, pairs), block(frm), :]

    def straight(self, k, w, frm, part):
        return remote(
            self.tile(k, w, part),
            self.slot(self.targets[k], frm, part),
            self.send.at[k, w, part],
            self.recv.at[k, frm, part],
            (self.oj, self.oi, w),
        )

    def detour(self, k, w, part):
        return remote(
            self.tile(k, w, part),
            self.slot(self.holds[k], self.v, part),
            self.send.at[k, w, part],
            self.hold_recv.at[k, self.v, part],
            (self.oj, self.oj, w),
        )

    def forward(self, k, frm, part, last):
        return remote(
            self.slot(self.holds[k], frm, part),
            self.slot((self.targets if last else self.holds)[k], frm, part),
            self.forward_send.at[k, frm, part],
            (self.recv if last else self.hold_recv).at[k, frm, part],
            (self.oi, (self.oi + 2) % 4 if last else 3 - self.oi, self.v),
        )

    def own(self, k):
        return pltpu.make_async_copy(
            self.sources[k].at[:, :, block(self.v)], self.targets[k].at[:, block(self.v), :], self.own_sem.at[k]
        )

    def goal(self, j):
        return ring_place(self.v, *ORDER[j])

    def came(self, j):
        return ring_place(self.v, -ORDER[j][0], -ORDER[j][1])

    def start(self, k, j):
        w = self.goal(j)

        def straight():
            for part in range(PARTS):
                self.straight(k, w, self.v, part).start()

        if j < RELAYED:
            pl.when(jnp.logical_not(self.apart))(straight)

            @pl.when(self.apart)
            def _():
                for part in range(PARTS):
                    self.detour(k, w, part).start()

        elif j < len(ORDER) - 1:
            straight()
        else:
            pl.when(jnp.logical_not(self.same))(straight)
            pl.when(self.same)(lambda: self.own(k).start())

    def relay(self, k, j):
        frm = self.came(j)
        for part in range(PARTS):

            @pl.when(self.same)
            def _():
                self.forward(k, frm, part, False).wait_recv()
                self.forward(k, frm, part, False).start()

            @pl.when(self.cross)
            def _():
                self.forward(k, frm, part, False).wait_recv()
                self.forward(k, frm, part, True).start()

    def arrive(self, k, j):
        frm = self.came(j)

        def wait():
            for part in range(PARTS):
                self.straight(k, frm, frm, part).wait_recv()

        if j < len(ORDER) - 1:
            wait()
        else:
            pl.when(self.same)(lambda: self.own(k).wait())
            pl.when(jnp.logical_not(self.same))(wait)

    def drain(self, k):
        for j in range(len(ORDER)):

            def sent():
                for part in range(PARTS):
                    self.straight(k, self.goal(j), self.v, part).wait_send()

            if j < len(ORDER) - 1:
                sent()
            else:
                pl.when(jnp.logical_not(self.same))(sent)
            if j < RELAYED:

                @pl.when(self.same | self.cross)
                def _():
                    for part in range(PARTS):
                        self.forward(k, self.came(j), part, True).wait_send()


def turn_sems(count):
    return [pltpu.SemaphoreType.DMA((count, 8, PARTS))] * 4 + [pltpu.SemaphoreType.DMA((count,))]


class Reduce:
    def __init__(self, p, d, acc, core_got, got1, got2, sems):
        self.p, self.d, self.acc, self.core_got, self.got1, self.got2 = p, d, acc, core_got, got1, got2
        self.core_sems, self.one_sems, self.plane_sems = sems
        oi, oj, v = places()
        self.core = oi % 2
        self.at = [v % 4, oj, (v // 4) * 2 + oi // 2]

    def device(self, core, at):
        x, y, z = at
        return (z % 2) * 2 + core, y, (z // 2) * 4 + x

    def shifted(self, moves):
        return self.device(self.core, [(p + moves.get(a, 0)) % 4 for a, p in enumerate(self.at)])

    def peers(self):
        found = [self.device(1 - self.core, self.at)]
        for dx in range(4):
            for dy in range(4):
                for dz in range(4):
                    if 0 in (dx, dy, dz) and (dx, dy, dz) != (0, 0, 0):
                        found.append(self.shifted({0: dx, 1: dy, 2: dz}))
        return found

    def columns(self, g):
        return pl.ds(*COLORS[g])

    def swap(self, g, back, here=True):
        sem = self.core_sems.at[back]
        twin = self.device(1 - self.core, self.at)
        if back:
            part = self.d.at[rows8((self.core if here else 1 - self.core) * 512, 512), self.columns(g)]
            return remote(part, part, sem.at[0, g], sem.at[1, g], twin)
        source = self.p.at[rows8((1 - self.core) * 512, 512), self.columns(g)]
        return remote(source, self.core_got.at[:, self.columns(g)], sem.at[0, g], sem.at[1, g], twin)

    def first(self, g, offset=0):
        return (self.at[g] + offset) % 4

    def rest(self, g, d2=0, d3=0):
        return ((self.at[(g + 1) % 3] + d2) % 4) * 4 + (self.at[(g + 2) % 3] + d3) % 4

    def one_axis(self, g, n, back, landed=False):
        sem = self.one_sems.at[back]
        peer = self.shifted({g: n})
        if back:
            place = self.first(g, -n if landed else 0)
            part = self.d.at[rows8(self.core * 512 + place * 128, 128), self.columns(g)]
            return remote(part, part, sem.at[0, g, n], sem.at[1, g, n], peer)
        source = self.acc.at[rows8(self.first(g, n) * 128, 128), self.columns(g)]
        return remote(source, self.got1.at[n - 1, :, self.columns(g)], sem.at[0, g, n], sem.at[1, g, n], peer)

    def plane(self, g, d2, d3, back, landed=False):
        n = d2 * 4 + d3
        sem = self.plane_sems.at[back]
        peer = self.shifted({(g + 1) % 3: d2, (g + 2) % 3: d3})
        if back:
            place = self.rest(g, -d2, -d3) if landed else self.rest(g)
            part = self.d.at[rows8(self.core * 512 + self.first(g) * 128 + place * 8, 8), self.columns(g)]
            return remote(part, part, sem.at[0, g, n], sem.at[1, g, n], peer)
        source = self.acc.at[rows8(self.first(g) * 128 + self.rest(g, d2, d3) * 8, 8), self.columns(g)]
        return remote(source, self.got2.at[n, :, self.columns(g)], sem.at[0, g, n], sem.at[1, g, n], peer)


AXIS = (2, 1, 3)
PLANE = sorted(((a, b) for a in range(4) for b in range(4) if a or b), key=lambda m: -sum((0, 1, 2, 1)[n] for n in m))
SWAP = (0, 2, 1, 3)


def kernel(
    x_ref, g_ref, fock_ref, kept_ref, out_ref,
    xm, xt, gt, xhold, ghold, z_ref, zt, zhold,
    g_top, g_rest, y_top, y_rest, p_ref, d_ref, acc, core_got, got1, got2,
    *sems,
):
    early = Turn([g_ref, xm], [gt, xt], [ghold, xhold], sems[:5])
    late = Turn([z_ref], [zt], [zhold], sems[5:10])
    reduce = Reduce(p_ref, d_ref, acc, core_got, got1, got2, sems[10:])
    oi, oj, v = places()
    core, half, x = oi % 2, v // 4, v % 4
    early.greet(reduce.peers())

    for j in range(8):
        early.start(0, j)
    for t in range(8):
        keep = kept_ref[v, t].astype(jnp.float32)
        columns = slice(t * BLK, t * BLK + BLK)
        xm[:, :, columns] = x_ref[:, :, columns] * keep
    for j in range(8):
        early.start(1, j)

    def halves(source, w):
        tile = source[:, block(w), :]
        return split(jnp.concatenate([tile[n] for n in range(4)], axis=1))

    for k in range(2):
        for j in range(RELAYED):
            early.relay(k, j)
    for j in range(8):
        early.arrive(0, j)
        w = early.came(j)
        g_top[block(w), :], g_rest[block(w), :] = halves(gt, w)
    for j in range(8):
        early.arrive(1, j)
        w = early.came(j)
        p_ref[block(w), :] = product(halves(xt, w), (g_top[...], g_rest[...]))

    def mixed(t):
        columns = slice(t * BLK, t * BLK + BLK)
        for n in range(4):
            both = xm[n, :, columns] + xt[SWAP[n], columns, :].T
            y_top[n * BLK : n * BLK + BLK, columns], y_rest[n * BLK : n * BLK + BLK, columns] = split(both)

    colours = range(3)
    for g in colours:
        reduce.swap(g, 0).start()
    mixed(0)
    for g in colours:
        at = reduce.columns(g)
        reduce.swap(g, 0).wait_recv()
        acc[:, at] = p_ref[rows8(core * 512, 512), at] + core_got[:, at]

        @pl.when((oj == 0) & (oi == half))
        def _():
            acc[block(x), at] -= fock_ref[:, at]

        for n in AXIS:
            reduce.one_axis(g, n, 0).start()
    mixed(1)
    mixed(2)
    mixed(3)
    for g in colours:
        at = reduce.columns(g)
        for n in AXIS:
            reduce.one_axis(g, n, 0).wait_recv()
        here = block(reduce.first(g))
        acc[here, at] = (acc[here, at] + got1[0, :, at]) + (got1[1, :, at] + got1[2, :, at])
        for move in PLANE:
            reduce.plane(g, *move, 0).start()
    mixed(4)
    mixed(5)
    for g in colours:
        at = reduce.columns(g)
        mine = reduce.first(g) * 128 + reduce.rest(g) * 8
        total = acc[rows8(mine, 8), at]
        for move in PLANE:
            reduce.plane(g, *move, 0).wait_recv()
            total = total + got2[move[0] * 4 + move[1], :, at]
        d_ref[rows8(core * 512 + mine, 8), at] = -total
        for move in PLANE:
            reduce.plane(g, *move, 1).start()
    mixed(6)
    mixed(7)
    for g in colours:
        for move in PLANE:
            reduce.plane(g, *move, 1, True).wait_recv()
        for n in AXIS:
            reduce.one_axis(g, n, 1).start()
    for g in colours:
        for n in AXIS:
            reduce.one_axis(g, n, 1, True).wait_recv()
        reduce.swap(g, 1).start()
    for g in colours:
        reduce.swap(g, 1, False).wait_recv()

    for j in range(0, 8, 2):
        ws = [late.goal(j), late.goal(j + 1)]
        d_rows = jnp.concatenate([d_ref[block(w), :] for w in ws], axis=0)
        part = product((y_top[...], y_rest[...]), split(d_rows))
        for m, w in enumerate(ws):
            for n in range(4):
                z_ref[n, :, block(w)] = part[n * BLK : n * BLK + BLK, m * BLK : m * BLK + BLK]
            late.start(0, j + m)
        if j >= 4:
            late.relay(0, j - 4)
            late.relay(0, j - 3)
    for j in range(8):
        late.arrive(0, j)
        w = late.came(j)
        for n in range(4):
            out_ref[n, :, block(w)] = z_ref[n, :, block(w)] + zt[SWAP[n], block(w), :].T

    early.drain(0)
    early.drain(1)
    late.drain(0)
    for back in range(2):
        for g in colours:
            reduce.swap(g, back).wait_send()
            for n in AXIS:
                reduce.one_axis(g, n, back).wait_send()
            for move in PLANE:
                reduce.plane(g, *move, back).wait_send()


def body(amplitudes, integrals, fock_virtual, screening):
    shape = amplitudes.shape
    rows, width = shape[2:]
    pairs = shape[0] * shape[1]
    f32, bf16 = jnp.float32, jnp.bfloat16
    vmem = pl.BlockSpec(memory_space=pltpu.VMEM)
    lying, standing = pltpu.VMEM((pairs, rows, width), f32), pltpu.VMEM((pairs, width, rows), f32)
    dma = pltpu.SemaphoreType.DMA
    out = pl.pallas_call(
        kernel,
        out_shape=jax.ShapeDtypeStruct((pairs, rows, width), f32),
        in_specs=[vmem] * 3 + [pl.BlockSpec(memory_space=pltpu.SMEM)],
        out_specs=vmem,
        scratch_shapes=[lying]
        + [standing] * 4
        + [lying]
        + [standing] * 2
        + [pltpu.VMEM((width, pairs * rows), bf16)] * 2
        + [pltpu.VMEM((pairs * rows, width), bf16)] * 2
        + [pltpu.VMEM((width, width), f32)] * 2
        + [pltpu.VMEM((width // 2, width), f32)] * 2
        + [pltpu.VMEM((3, 128, width), f32), pltpu.VMEM((16, 8, width), f32)]
        + turn_sems(2)
        + turn_sems(1)
        + [dma((2, 2, 3)), dma((2, 2, 3, 4)), dma((2, 2, 3, 16))],
        compiler_params=pltpu.CompilerParams(collective_id=1, has_side_effects=True, vmem_limit_bytes=60 * 2**20),
        name="residual",
    )(
        amplitudes.reshape(pairs, rows, width),
        integrals.reshape(pairs, rows, width),
        fock_virtual,
        screening.reshape(screening.shape[2:]),
    )
    return out.reshape(shape)


def solution(mesh):
    placed = (
        P("oi", "oj", "vir", None),
        P("oi", "oj", "vir", None),
        P("vir", None),
        P("oi", "oj", None, None),
    )
    return jax.shard_map(
        body, mesh=mesh, in_specs=placed, out_specs=P("oi", "oj", "vir", None), check_vma=False
    )
```

```python
import functools

import jax
import jax.numpy as jnp
from jax import lax
from jax.experimental import pallas as pl
from jax.experimental.pallas import tpu as pltpu
from jax.sharding import PartitionSpec as P

BLK = 128
MESH = pl.DeviceIdType.MESH
COLORS = ((0, 256), (256, 256), (512, 256), (768, 128), (896, 128))
ORDER = ((0, 2), (1, 2), (0, 1), (0, 3), (1, 1), (1, 3), (1, 0), (0, 0))
RELAYED = 4
PARTS = 1
NT = (((1,), (1,)), ((), ()))


def places():
    return lax.axis_index("oi"), lax.axis_index("oj"), lax.axis_index("vir")


def ring_place(v, dh, dx):
    return ((v // 4 + dh % 2) % 2) * 4 + (v % 4 + dx % 4) % 4


def block(w):
    return pl.ds(pl.multiple_of(w * BLK, BLK), BLK)


def rows8(start, size):
    return pl.ds(pl.multiple_of(start, 8), size)


def split(values):
    top = values.astype(jnp.bfloat16)
    return top, (values - top.astype(jnp.float32)).astype(jnp.bfloat16)


def product(a, b):
    (a1, a2), (b1, b2) = a, b
    dot = functools.partial(lax.dot_general, dimension_numbers=NT, preferred_element_type=jnp.float32)
    return dot(a1, b1) + (dot(a1, b2) + dot(a2, b1))


def remote(source, target, send, recv, peer):
    return pltpu.make_async_remote_copy(
        src_ref=source, dst_ref=target, send_sem=send, recv_sem=recv, device_id=peer, device_id_type=MESH
    )


class Turn:
    def __init__(self, sources, targets, holds, sems):
        self.sources, self.targets, self.holds = sources, targets, holds
        self.send, self.recv, self.hold_recv, self.forward_send, self.own_sem = sems
        self.oi, self.oj, self.v = places()
        self.same = self.oi == self.oj
        self.apart = (self.oi + 2) % 4 == self.oj
        self.cross = self.oi + self.oj == 3

    def greet(self, more):
        oi, oj, v = self.oi, self.oj, self.v
        barrier = pltpu.get_barrier_semaphore()

        def signal(*peers):
            for peer in peers:
                pl.semaphore_signal(barrier, inc=1, device_id=peer, device_id_type=MESH)

        def everyone(a, b):
            return [(a, b, ring_place(v, dh, dx)) for dh, dx in ORDER]

        signal(*more, *everyone(oj, oi)[:-1])

        @pl.when(jnp.logical_not(self.same))
        def _():
            signal((oj, oi, v))

        @pl.when(self.same)
        def _():
            signal(*everyone((oi + 2) % 4, oi), (oi, 3 - oi, v))

        @pl.when(self.apart)
        def _():
            signal(*everyone(oj, oj), (oi, 3 - oi, v))

        @pl.when(self.cross)
        def _():
            signal((oi, oi, v), (oi, (oi + 2) % 4, v))

        kinds = jnp.where(self.same, 16, jnp.where(self.apart, 17, jnp.where(self.cross, 10, 8)))
        pl.semaphore_wait(barrier, kinds + len(more))

    def tile(self, k, w, part):
        pairs = self.sources[k].shape[0] // PARTS
        return self.sources[k].at[pl.ds(part * pairs, pairs), :, block(w)]

    def slot(self, array, frm, part):
        pairs = array.shape[0] // PARTS
        return array.at[pl.ds(part * pairs, pairs), block(frm), :]

    def straight(self, k, w, frm, part):
        return remote(
            self.tile(k, w, part),
            self.slot(self.targets[k], frm, part),
            self.send.at[k, w, part],
            self.recv.at[k, frm, part],
            (self.oj, self.oi, w),
        )

    def detour(self, k, w, part):
        return remote(
            self.tile(k, w, part),
            self.slot(self.holds[k], self.v, part),
            self.send.at[k, w, part],
            self.hold_recv.at[k, self.v, part],
            (self.oj, self.oj, w),
        )

    def forward(self, k, frm, part, last):
        return remote(
            self.slot(self.holds[k], frm, part),
            self.slot((self.targets if last else self.holds)[k], frm, part),
            self.forward_send.at[k, frm, part],
            (self.recv if last else self.hold_recv).at[k, frm, part],
            (self.oi, (self.oi + 2) % 4 if last else 3 - self.oi, self.v),
        )

    def own(self, k):
        return pltpu.make_async_copy(
            self.sources[k].at[:, :, block(self.v)], self.targets[k].at[:, block(self.v), :], self.own_sem.at[k]
        )

    def goal(self, j):
        return ring_place(self.v, *ORDER[j])

    def came(self, j):
        return ring_place(self.v, -ORDER[j][0], -ORDER[j][1])

    def start(self, k, j):
        w = self.goal(j)

        def straight():
            for part in range(PARTS):
                self.straight(k, w, self.v, part).start()

        if j < RELAYED:
            pl.when(jnp.logical_not(self.apart))(straight)

            @pl.when(self.apart)
            def _():
                for part in range(PARTS):
                    self.detour(k, w, part).start()

        elif j < len(ORDER) - 1:
            straight()
        else:
            pl.when(jnp.logical_not(self.same))(straight)
            pl.when(self.same)(lambda: self.own(k).start())

    def relay(self, k, j):
        frm = self.came(j)
        for part in range(PARTS):

            @pl.when(self.same)
            def _():
                self.forward(k, frm, part, False).wait_recv()
                self.forward(k, frm, part, False).start()

            @pl.when(self.cross)
            def _():
                self.forward(k, frm, part, False).wait_recv()
                self.forward(k, frm, part, True).start()

    def arrive(self, k, j):
        frm = self.came(j)

        def wait():
            for part in range(PARTS):
                self.straight(k, frm, frm, part).wait_recv()

        if j < len(ORDER) - 1:
            wait()
        else:
            pl.when(self.same)(lambda: self.own(k).wait())
            pl.when(jnp.logical_not(self.same))(wait)

    def drain(self, k):
        for j in range(len(ORDER)):

            def sent():
                for part in range(PARTS):
                    self.straight(k, self.goal(j), self.v, part).wait_send()

            if j < len(ORDER) - 1:
                sent()
            else:
                pl.when(jnp.logical_not(self.same))(sent)
            if j < RELAYED:

                @pl.when(self.same | self.cross)
                def _():
                    for part in range(PARTS):
                        self.forward(k, self.came(j), part, True).wait_send()


def turn_sems(count):
    return [pltpu.SemaphoreType.DMA((count, 8, PARTS))] * 4 + [pltpu.SemaphoreType.DMA((count,))]


class Reduce:
    def __init__(self, p, d, acc, core_got, got1, got2, sems):
        self.p, self.d, self.acc, self.core_got, self.got1, self.got2 = p, d, acc, core_got, got1, got2
        self.give_sems, self.back_sems, self.one_sems, self.plane_sems = sems
        oi, oj, v = places()
        self.core = oi % 2
        self.at = [v % 4, oj, (v // 4) * 2 + oi // 2]

    def device(self, core, at):
        x, y, z = at
        return (z % 2) * 2 + core, y, (z // 2) * 4 + x

    def shifted(self, moves):
        return self.device(self.core, [(p + moves.get(a, 0)) % 4 for a, p in enumerate(self.at)])

    def peers(self):
        found = [self.device(1 - self.core, self.at)]
        for dx in range(4):
            for dy in range(4):
                for dz in range(4):
                    if 0 in (dx, dy, dz) and (dx, dy, dz) != (0, 0, 0):
                        found.append(self.shifted({0: dx, 1: dy, 2: dz}))
        return found

    def columns(self, g):
        return pl.ds(*COLORS[g])

    def give(self, w):
        q = w % 4
        twin = self.device(1 - self.core, self.at)
        return remote(self.p.at[block(w)], self.core_got.at[block(q)], self.give_sems.at[0, q], self.give_sems.at[1, q], twin)

    def give_back(self, g, q, here=True):
        half = self.core if here else 1 - self.core
        part = self.d.at[block(half * 4 + q), self.columns(g)]
        sems = self.back_sems
        return remote(part, part, sems.at[0, g, q], sems.at[1, g, q], self.device(1 - self.core, self.at))

    def send_block(self, g, q):
        n = (q + 4 - self.at[g % 3]) % 4
        sems = self.one_sems.at[0]
        at = list(self.at)
        at[g % 3] = q

        @pl.when(n != 0)
        def _():
            remote(
                self.acc.at[block(q), self.columns(g)],
                self.got1.at[n - 1, :, self.columns(g)],
                sems.at[0, g, n],
                sems.at[1, g, n],
                self.device(self.core, at),
            ).start()

    def first(self, g, offset=0):
        return (self.at[g % 3] + offset) % 4

    def rest(self, g, d2=0, d3=0):
        return ((self.at[(g + 1) % 3] + d2) % 4) * 4 + (self.at[(g + 2) % 3] + d3) % 4

    def one_axis(self, g, n, back, landed=False):
        sem = self.one_sems.at[back]
        peer = self.shifted({g % 3: n})
        if back:
            place = self.first(g, -n if landed else 0)
            part = self.d.at[rows8(self.core * 512 + place * 128, 128), self.columns(g)]
            return remote(part, part, sem.at[0, g, n], sem.at[1, g, n], peer)
        source = self.acc.at[rows8(self.first(g, n) * 128, 128), self.columns(g)]
        return remote(source, self.got1.at[n - 1, :, self.columns(g)], sem.at[0, g, n], sem.at[1, g, n], peer)

    def plane(self, g, d2, d3, back, landed=False):
        n = d2 * 4 + d3
        sem = self.plane_sems.at[back]
        peer = self.shifted({(g + 1) % 3: d2, (g + 2) % 3: d3})
        if back:
            place = self.rest(g, -d2, -d3) if landed else self.rest(g)
            part = self.d.at[rows8(self.core * 512 + self.first(g) * 128 + place * 8, 8), self.columns(g)]
            return remote(part, part, sem.at[0, g, n], sem.at[1, g, n], peer)
        source = self.acc.at[rows8(self.first(g) * 128 + self.rest(g, d2, d3) * 8, 8), self.columns(g)]
        return remote(source, self.got2.at[n, :, self.columns(g)], sem.at[0, g, n], sem.at[1, g, n], peer)


AXIS = (2, 1, 3)
PLANE = sorted(((a, b) for a in range(4) for b in range(4) if a or b), key=lambda m: -sum((0, 1, 2, 1)[n] for n in m))
SWAP = (0, 2, 1, 3)


def kernel(
    x_far, g_ref, fock_far, kept_ref, out_far,
    out_ref, store_sem, x_ref, fock_ref, load_sem, xm, xt, gt, xhold, ghold, z_ref, zt, zhold,
    g_top, g_rest, y_top, y_rest, p_ref, d_ref, acc, core_got, got1, got2,
    *sems,
):
    early = Turn([g_ref, xm], [gt, xt], [ghold, xhold], sems[:5])
    late = Turn([z_ref], [zt], [zhold], sems[5:10])
    reduce = Reduce(p_ref, d_ref, acc, core_got, got1, got2, sems[10:])
    oi, oj, v = places()
    core, half = oi % 2, v // 4
    loads = [
        pltpu.make_async_copy(x_far, x_ref, load_sem.at[0]),
        pltpu.make_async_copy(fock_far, fock_ref, load_sem.at[1]),
    ]
    for load in loads:
        load.start()
    early.greet(reduce.peers())

    for j in range(8):
        early.start(0, j)
    for load in loads:
        load.wait()
    for t in range(8):
        keep = kept_ref[v, t].astype(jnp.float32)
        columns = slice(t * BLK, t * BLK + BLK)
        xm[:, :, columns] = x_ref[:, :, columns] * keep
    for j in range(8):
        early.start(1, j)

    def halves(source, w):
        tile = source[:, block(w), :]
        return split(jnp.concatenate([tile[n] for n in range(4)], axis=1))

    for k in range(2):
        for j in range(RELAYED):
            early.relay(k, j)
    for j in range(8):
        early.arrive(0, j)
        w = early.came(j)
        g_top[block(w), :], g_rest[block(w), :] = halves(gt, w)

    def take(j):
        w = early.came(j)
        q = w % 4

        @pl.when(w // 4 == core)
        def _():
            reduce.give(w).wait_recv()
            acc[block(q), :] = p_ref[block(w), :] + core_got[block(q), :]
            if j == 7:

                @pl.when((oj == 0) & (oi == half))
                def _():
                    acc[block(q), :] -= fock_ref[...]

            for g in range(len(COLORS)):
                reduce.send_block(g, q)

    for j in range(8):
        early.arrive(1, j)
        w = early.came(j)
        p_ref[block(w), :] = product(halves(xt, w), (g_top[...], g_rest[...]))
        pl.when(w // 4 != core)(lambda: reduce.give(w).start())
        if j:
            take(j - 1)

    def mixed(t):
        columns = slice(t * BLK, t * BLK + BLK)
        for n in range(4):
            both = xm[n, :, columns] + xt[SWAP[n], columns, :].T
            y_top[n * BLK : n * BLK + BLK, columns], y_rest[n * BLK : n * BLK + BLK, columns] = split(both)

    colours = range(len(COLORS))
    mixed(0)
    take(7)
    mixed(1)
    mixed(2)
    mixed(3)
    for g in colours:
        at = reduce.columns(g)
        for n in AXIS:
            reduce.one_axis(g, n, 0).wait_recv()
        here = block(reduce.first(g))
        acc[here, at] = (acc[here, at] + got1[0, :, at]) + (got1[1, :, at] + got1[2, :, at])
        for move in PLANE:
            reduce.plane(g, *move, 0).start()
    mixed(4)
    mixed(5)
    for g in colours:
        at = reduce.columns(g)
        mine = reduce.first(g) * 128 + reduce.rest(g) * 8
        total = acc[rows8(mine, 8), at]
        for move in PLANE:
            reduce.plane(g, *move, 0).wait_recv()
            total = total + got2[move[0] * 4 + move[1], :, at]
        d_ref[rows8(core * 512 + mine, 8), at] = -total
        for move in PLANE:
            reduce.plane(g, *move, 1).start()
    mixed(6)
    mixed(7)
    for g in colours:
        for move in PLANE:
            reduce.plane(g, *move, 1, True).wait_recv()
        for n in AXIS:
            reduce.one_axis(g, n, 1).start()
        reduce.give_back(g, reduce.first(g)).start()
    for n in (1, 3, 2):
        for g in colours:
            reduce.one_axis(g, n, 1, True).wait_recv()
            reduce.give_back(g, reduce.first(g, -n)).start()
    for g in colours:
        for q in range(4):
            reduce.give_back(g, q, False).wait_recv()

    for j in range(0, 8, 2):
        ws = [late.goal(j), late.goal(j + 1)]
        d_rows = jnp.concatenate([d_ref[block(w), :] for w in ws], axis=0)
        part = product((y_top[...], y_rest[...]), split(d_rows))
        for m, w in enumerate(ws):
            for n in range(4):
                z_ref[n, :, block(w)] = part[n * BLK : n * BLK + BLK, m * BLK : m * BLK + BLK]
            late.start(0, j + m)
        if j >= 4:
            late.relay(0, j - 4)
            late.relay(0, j - 3)
    for j in range(8):
        late.arrive(0, j)
        w = late.came(j)
        for n in range(4):
            out_ref[n, :, block(w)] = z_ref[n, :, block(w)] + zt[SWAP[n], block(w), :].T
        pltpu.make_async_copy(out_ref.at[:, :, block(w)], out_far.at[:, :, block(w)], store_sem.at[j]).start()

    early.drain(0)
    early.drain(1)
    late.drain(0)
    for j in range(8):
        w = late.came(j)
        pltpu.make_async_copy(out_ref.at[:, :, block(w)], out_far.at[:, :, block(w)], store_sem.at[j]).wait()
    for q in range(4):
        reduce.give(q).wait_send()
        for g in colours:
            reduce.give_back(g, q).wait_send()
    for back in range(2):
        for g in colours:
            for n in AXIS:
                reduce.one_axis(g, n, back).wait_send()
            for move in PLANE:
                reduce.plane(g, *move, back).wait_send()


def body(amplitudes, integrals, fock_virtual, screening):
    shape = amplitudes.shape
    rows, width = shape[2:]
    pairs = shape[0] * shape[1]
    f32, bf16 = jnp.float32, jnp.bfloat16
    lying, standing = pltpu.VMEM((pairs, rows, width), f32), pltpu.VMEM((pairs, width, rows), f32)
    dma = pltpu.SemaphoreType.DMA
    out = pl.pallas_call(
        kernel,
        out_shape=jax.ShapeDtypeStruct((pairs, rows, width), f32),
        in_specs=[pl.BlockSpec(memory_space=pl.ANY)] * 3 + [pl.BlockSpec(memory_space=pltpu.SMEM)],
        out_specs=pl.BlockSpec(memory_space=pl.ANY),
        scratch_shapes=[lying, dma((8,)), lying, pltpu.VMEM((rows, width), f32), dma((2,)), lying]
        + [standing] * 4
        + [lying]
        + [standing] * 2
        + [pltpu.VMEM((width, pairs * rows), bf16)] * 2
        + [pltpu.VMEM((pairs * rows, width), bf16)] * 2
        + [pltpu.VMEM((width, width), f32)] * 2
        + [pltpu.VMEM((width // 2, width), f32)] * 2
        + [pltpu.VMEM((3, 128, width), f32), pltpu.VMEM((16, 8, width), f32)]
        + turn_sems(2)
        + turn_sems(1)
        + [dma((2, 4))]
        + [dma((2, len(COLORS), 4)), dma((2, 2, len(COLORS), 4)), dma((2, 2, len(COLORS), 16))],
        compiler_params=pltpu.CompilerParams(collective_id=1, has_side_effects=True, vmem_limit_bytes=60 * 2**20),
        name="residual",
    )(
        amplitudes.reshape(pairs, rows, width),
        integrals.reshape(pairs, rows, width),
        fock_virtual,
        screening.reshape(screening.shape[2:]),
    )
    return out.reshape(shape)


def solution(mesh):
    placed = (
        P("oi", "oj", "vir", None),
        P("oi", "oj", "vir", None),
        P("vir", None),
        P("oi", "oj", None, None),
    )
    return jax.shard_map(
        body, mesh=mesh, in_specs=placed, out_specs=P("oi", "oj", "vir", None), check_vma=False
    )
```

```python
import functools

import jax
import jax.numpy as jnp
from jax import lax
from jax.experimental import pallas as pl
from jax.experimental.pallas import tpu as pltpu
from jax.sharding import PartitionSpec as P

BLK = 128
MESH = pl.DeviceIdType.MESH
COLORS = ((0, 256), (256, 256), (512, 256), (768, 128), (896, 128))
ORDER = ((0, 2), (1, 2), (0, 1), (0, 3), (1, 1), (1, 3), (1, 0), (0, 0))
RELAYED = 4
PARTS = 1
NT = (((1,), (1,)), ((), ()))


def places():
    return lax.axis_index("oi"), lax.axis_index("oj"), lax.axis_index("vir")


def ring_place(v, dh, dx):
    return ((v // 4 + dh % 2) % 2) * 4 + (v % 4 + dx % 4) % 4


def block(w):
    return pl.ds(pl.multiple_of(w * BLK, BLK), BLK)


def rows8(start, size):
    return pl.ds(pl.multiple_of(start, 8), size)


def split(values):
    top = values.astype(jnp.bfloat16)
    return top, (values - top.astype(jnp.float32)).astype(jnp.bfloat16)


def product(a, b):
    (a1, a2), (b1, b2) = a, b
    dot = functools.partial(lax.dot_general, dimension_numbers=NT, preferred_element_type=jnp.float32)
    return dot(a1, b1) + (dot(a1, b2) + dot(a2, b1))


def remote(source, target, send, recv, peer):
    return pltpu.make_async_remote_copy(
        src_ref=source, dst_ref=target, send_sem=send, recv_sem=recv, device_id=peer, device_id_type=MESH
    )


class Turn:
    def __init__(self, sources, targets, holds, sems):
        self.sources, self.targets, self.holds = sources, targets, holds
        self.send, self.recv, self.hold_recv, self.forward_send, self.own_sem = sems
        self.oi, self.oj, self.v = places()
        self.same = self.oi == self.oj
        self.apart = (self.oi + 2) % 4 == self.oj
        self.cross = self.oi + self.oj == 3

    def greet(self, more):
        oi, oj, v = self.oi, self.oj, self.v
        barrier = pltpu.get_barrier_semaphore()

        def signal(*peers):
            for peer in peers:
                pl.semaphore_signal(barrier, inc=1, device_id=peer, device_id_type=MESH)

        def everyone(a, b):
            return [(a, b, ring_place(v, dh, dx)) for dh, dx in ORDER]

        signal(*more, *everyone(oj, oi)[:-1])

        @pl.when(jnp.logical_not(self.same))
        def _():
            signal((oj, oi, v))

        @pl.when(self.same)
        def _():
            signal(*everyone((oi + 2) % 4, oi), (oi, 3 - oi, v))

        @pl.when(self.apart)
        def _():
            signal(*everyone(oj, oj), (oi, 3 - oi, v))

        @pl.when(self.cross)
        def _():
            signal((oi, oi, v), (oi, (oi + 2) % 4, v))

        kinds = jnp.where(self.same, 16, jnp.where(self.apart, 17, jnp.where(self.cross, 10, 8)))
        pl.semaphore_wait(barrier, kinds + len(more))

    def tile(self, k, w, part):
        pairs = self.sources[k].shape[0] // PARTS
        return self.sources[k].at[pl.ds(part * pairs, pairs), :, block(w)]

    def slot(self, array, frm, part):
        pairs = array.shape[0] // PARTS
        return array.at[pl.ds(part * pairs, pairs), block(frm), :]

    def straight(self, k, w, frm, part):
        return remote(
            self.tile(k, w, part),
            self.slot(self.targets[k], frm, part),
            self.send.at[k, w, part],
            self.recv.at[k, frm, part],
            (self.oj, self.oi, w),
        )

    def detour(self, k, w, part):
        return remote(
            self.tile(k, w, part),
            self.slot(self.holds[k], self.v, part),
            self.send.at[k, w, part],
            self.hold_recv.at[k, self.v, part],
            (self.oj, self.oj, w),
        )

    def forward(self, k, frm, part, last):
        return remote(
            self.slot(self.holds[k], frm, part),
            self.slot((self.targets if last else self.holds)[k], frm, part),
            self.forward_send.at[k, frm, part],
            (self.recv if last else self.hold_recv).at[k, frm, part],
            (self.oi, (self.oi + 2) % 4 if last else 3 - self.oi, self.v),
        )

    def own(self, k):
        return pltpu.make_async_copy(
            self.sources[k].at[:, :, block(self.v)], self.targets[k].at[:, block(self.v), :], self.own_sem.at[k]
        )

    def goal(self, j):
        return ring_place(self.v, *ORDER[j])

    def came(self, j):
        return ring_place(self.v, -ORDER[j][0], -ORDER[j][1])

    def start(self, k, j):
        w = self.goal(j)

        def straight():
            for part in range(PARTS):
                self.straight(k, w, self.v, part).start()

        if j < RELAYED:
            pl.when(jnp.logical_not(self.apart))(straight)

            @pl.when(self.apart)
            def _():
                for part in range(PARTS):
                    self.detour(k, w, part).start()

        elif j < len(ORDER) - 1:
            straight()
        else:
            pl.when(jnp.logical_not(self.same))(straight)
            pl.when(self.same)(lambda: self.own(k).start())

    def relay(self, k, j):
        frm = self.came(j)
        for part in range(PARTS):

            @pl.when(self.same)
            def _():
                self.forward(k, frm, part, False).wait_recv()
                self.forward(k, frm, part, False).start()

            @pl.when(self.cross)
            def _():
                self.forward(k, frm, part, False).wait_recv()
                self.forward(k, frm, part, True).start()

    def arrive(self, k, j):
        frm = self.came(j)

        def wait():
            for part in range(PARTS):
                self.straight(k, frm, frm, part).wait_recv()

        if j < len(ORDER) - 1:
            wait()
        else:
            pl.when(self.same)(lambda: self.own(k).wait())
            pl.when(jnp.logical_not(self.same))(wait)

    def drain(self, k):
        for j in range(len(ORDER)):

            def sent():
                for part in range(PARTS):
                    self.straight(k, self.goal(j), self.v, part).wait_send()

            if j < len(ORDER) - 1:
                sent()
            else:
                pl.when(jnp.logical_not(self.same))(sent)
            if j < RELAYED:

                @pl.when(self.same | self.cross)
                def _():
                    for part in range(PARTS):
                        self.forward(k, self.came(j), part, True).wait_send()


def turn_sems(count):
    return [pltpu.SemaphoreType.DMA((count, 8, PARTS))] * 4 + [pltpu.SemaphoreType.DMA((count,))]


class Reduce:
    def __init__(self, p, d, acc, core_got, got1, got2, sems):
        self.p, self.d, self.acc, self.core_got, self.got1, self.got2 = p, d, acc, core_got, got1, got2
        self.give_sems, self.back_sems, self.one_sems, self.plane_sems = sems
        oi, oj, v = places()
        self.core = oi % 2
        self.at = [v % 4, oj, (v // 4) * 2 + oi // 2]

    def device(self, core, at):
        x, y, z = at
        return (z % 2) * 2 + core, y, (z // 2) * 4 + x

    def shifted(self, moves):
        return self.device(self.core, [(p + moves.get(a, 0)) % 4 for a, p in enumerate(self.at)])

    def peers(self):
        found = [self.device(1 - self.core, self.at)]
        for dx in range(4):
            for dy in range(4):
                for dz in range(4):
                    if 0 in (dx, dy, dz) and (dx, dy, dz) != (0, 0, 0):
                        found.append(self.shifted({0: dx, 1: dy, 2: dz}))
        return found

    def columns(self, g):
        return pl.ds(*COLORS[g])

    def give(self, w):
        q = w % 4
        twin = self.device(1 - self.core, self.at)
        return remote(self.p.at[block(w)], self.core_got.at[block(q)], self.give_sems.at[0, q], self.give_sems.at[1, q], twin)

    def give_back(self, g, q, here=True):
        half = self.core if here else 1 - self.core
        part = self.d.at[block(half * 4 + q), self.columns(g)]
        sems = self.back_sems
        return remote(part, part, sems.at[0, g, q], sems.at[1, g, q], self.device(1 - self.core, self.at))

    def send_block(self, g, q):
        n = (q + 4 - self.at[g % 3]) % 4
        sems = self.one_sems.at[0]
        at = list(self.at)
        at[g % 3] = q

        @pl.when(n != 0)
        def _():
            remote(
                self.acc.at[block(q), self.columns(g)],
                self.got1.at[n - 1, :, self.columns(g)],
                sems.at[0, g, n],
                sems.at[1, g, n],
                self.device(self.core, at),
            ).start()

    def first(self, g, offset=0):
        return (self.at[g % 3] + offset) % 4

    def rest(self, g, d2=0, d3=0):
        return ((self.at[(g + 1) % 3] + d2) % 4) * 4 + (self.at[(g + 2) % 3] + d3) % 4

    def one_axis(self, g, n, back, landed=False):
        sem = self.one_sems.at[back]
        peer = self.shifted({g % 3: n})
        if back:
            place = self.first(g, -n if landed else 0)
            part = self.d.at[rows8(self.core * 512 + place * 128, 128), self.columns(g)]
            return remote(part, part, sem.at[0, g, n], sem.at[1, g, n], peer)
        source = self.acc.at[rows8(self.first(g, n) * 128, 128), self.columns(g)]
        return remote(source, self.got1.at[n - 1, :, self.columns(g)], sem.at[0, g, n], sem.at[1, g, n], peer)

    def plane(self, g, d2, d3, back, landed=False):
        n = d2 * 4 + d3
        sem = self.plane_sems.at[back]
        peer = self.shifted({(g + 1) % 3: d2, (g + 2) % 3: d3})
        if back:
            place = self.rest(g, -d2, -d3) if landed else self.rest(g)
            part = self.d.at[rows8(self.core * 512 + self.first(g) * 128 + place * 8, 8), self.columns(g)]
            return remote(part, part, sem.at[0, g, n], sem.at[1, g, n], peer)
        source = self.acc.at[rows8(self.first(g) * 128 + self.rest(g, d2, d3) * 8, 8), self.columns(g)]
        return remote(source, self.got2.at[n, :, self.columns(g)], sem.at[0, g, n], sem.at[1, g, n], peer)


AXIS = (2, 1, 3)
PLANE = sorted(((a, b) for a in range(4) for b in range(4) if a or b), key=lambda m: -sum((0, 1, 2, 1)[n] for n in m))
SWAP = (0, 2, 1, 3)


def kernel(
    x_far, g_ref, fock_far, kept_ref, out_far,
    out_ref, store_sem, x_ref, fock_ref, load_sem, xm, xt, gt, xhold, ghold, z_ref, zt, zhold,
    g_top, g_rest, y_top, y_rest, p_ref, d_ref, acc, core_got, got1, got2,
    *sems,
):
    early = Turn([g_ref, xm], [gt, xt], [ghold, xhold], sems[:5])
    late = Turn([z_ref], [zt], [zhold], sems[5:10])
    reduce = Reduce(p_ref, d_ref, acc, core_got, got1, got2, sems[10:])
    oi, oj, v = places()
    core, half = oi % 2, v // 4
    loads = [
        pltpu.make_async_copy(x_far, x_ref, load_sem.at[0]),
        pltpu.make_async_copy(fock_far, fock_ref, load_sem.at[1]),
    ]
    for load in loads:
        load.start()
    early.greet(reduce.peers())

    for j in range(8):
        early.start(0, j)
    for load in loads:
        load.wait()
    for t in range(8):
        keep = kept_ref[v, t].astype(jnp.float32)
        columns = slice(t * BLK, t * BLK + BLK)
        xm[:, :, columns] = x_ref[:, :, columns] * keep
    for j in range(8):
        early.start(1, j)

    def halves(source, w):
        tile = source[:, block(w), :]
        return split(jnp.concatenate([tile[n] for n in range(4)], axis=1))

    for k in range(2):
        for j in range(RELAYED):
            early.relay(k, j)
    for j in range(8):
        early.arrive(0, j)
        w = early.came(j)
        g_top[block(w), :], g_rest[block(w), :] = halves(gt, w)

    def take(j):
        w = early.came(j)
        q = w % 4

        @pl.when(w // 4 == core)
        def _():
            reduce.give(w).wait_recv()
            acc[block(q), :] = p_ref[block(w), :] + core_got[block(q), :]
            if j == 7:

                @pl.when((oj == 0) & (oi == half))
                def _():
                    acc[block(q), :] -= fock_ref[...]

            for g in range(len(COLORS)):
                reduce.send_block(g, q)

    for j in range(8):
        early.arrive(1, j)
        w = early.came(j)
        p_ref[block(w), :] = product(halves(xt, w), (g_top[...], g_rest[...]))
        pl.when(w // 4 != core)(lambda: reduce.give(w).start())
        if j:
            take(j - 1)

    def mixed(t):
        columns = slice(t * BLK, t * BLK + BLK)
        for n in range(4):
            both = xm[n, :, columns] + xt[SWAP[n], columns, :].T
            y_top[n * BLK : n * BLK + BLK, columns], y_rest[n * BLK : n * BLK + BLK, columns] = split(both)

    colours = range(len(COLORS))
    mixed(0)
    take(7)
    mixed(1)
    mixed(2)
    mixed(3)
    for g in colours:
        at = reduce.columns(g)
        for n in AXIS:
            reduce.one_axis(g, n, 0).wait_recv()
        here = block(reduce.first(g))
        acc[here, at] = (acc[here, at] + got1[0, :, at]) + (got1[1, :, at] + got1[2, :, at])
        for move in PLANE:
            reduce.plane(g, *move, 0).start()
    mixed(4)
    mixed(5)
    for g in colours:
        at = reduce.columns(g)
        mine = reduce.first(g) * 128 + reduce.rest(g) * 8
        total = acc[rows8(mine, 8), at]
        for move in PLANE:
            reduce.plane(g, *move, 0).wait_recv()
            total = total + got2[move[0] * 4 + move[1], :, at]
        d_ref[rows8(core * 512 + mine, 8), at] = -total
        for move in PLANE:
            reduce.plane(g, *move, 1).start()
    mixed(6)
    mixed(7)
    for g in colours:
        for move in PLANE:
            reduce.plane(g, *move, 1, True).wait_recv()
        for n in AXIS:
            reduce.one_axis(g, n, 1).start()
        reduce.give_back(g, reduce.first(g)).start()
    for n in (1, 3, 2):
        for g in colours:
            reduce.one_axis(g, n, 1, True).wait_recv()
            reduce.give_back(g, reduce.first(g, -n)).start()
    for g in colours:
        for q in range(4):
            reduce.give_back(g, q, False).wait_recv()

    for j in range(0, 8, 2):
        ws = [late.goal(j), late.goal(j + 1)]
        d_rows = jnp.concatenate([d_ref[block(w), :] for w in ws], axis=0)
        part = product((y_top[...], y_rest[...]), split(d_rows))
        for m, w in enumerate(ws):
            for n in range(4):
                z_ref[n, :, block(w)] = part[n * BLK : n * BLK + BLK, m * BLK : m * BLK + BLK]
            late.start(0, j + m)
        if j == 2:
            late.relay(0, 0)
        if j == 4:
            late.relay(0, 1)
    late.relay(0, 2)
    late.relay(0, 3)
    for j in range(8):
        late.arrive(0, j)
        w = late.came(j)
        for n in range(4):
            out_ref[n, :, block(w)] = z_ref[n, :, block(w)] + zt[SWAP[n], block(w), :].T
        pltpu.make_async_copy(out_ref.at[:, :, block(w)], out_far.at[:, :, block(w)], store_sem.at[j]).start()

    early.drain(0)
    early.drain(1)
    late.drain(0)
    for j in range(8):
        w = late.came(j)
        pltpu.make_async_copy(out_ref.at[:, :, block(w)], out_far.at[:, :, block(w)], store_sem.at[j]).wait()
    for q in range(4):
        reduce.give(q).wait_send()
        for g in colours:
            reduce.give_back(g, q).wait_send()
    for back in range(2):
        for g in colours:
            for n in AXIS:
                reduce.one_axis(g, n, back).wait_send()
            for move in PLANE:
                reduce.plane(g, *move, back).wait_send()


def body(amplitudes, integrals, fock_virtual, screening):
    shape = amplitudes.shape
    rows, width = shape[2:]
    pairs = shape[0] * shape[1]
    f32, bf16 = jnp.float32, jnp.bfloat16
    lying, standing = pltpu.VMEM((pairs, rows, width), f32), pltpu.VMEM((pairs, width, rows), f32)
    dma = pltpu.SemaphoreType.DMA
    out = pl.pallas_call(
        kernel,
        out_shape=jax.ShapeDtypeStruct((pairs, rows, width), f32),
        in_specs=[pl.BlockSpec(memory_space=pl.ANY)] * 3 + [pl.BlockSpec(memory_space=pltpu.SMEM)],
        out_specs=pl.BlockSpec(memory_space=pl.ANY),
        scratch_shapes=[lying, dma((8,)), lying, pltpu.VMEM((rows, width), f32), dma((2,)), lying]
        + [standing] * 4
        + [lying]
        + [standing] * 2
        + [pltpu.VMEM((width, pairs * rows), bf16)] * 2
        + [pltpu.VMEM((pairs * rows, width), bf16)] * 2
        + [pltpu.VMEM((width, width), f32)] * 2
        + [pltpu.VMEM((width // 2, width), f32)] * 2
        + [pltpu.VMEM((3, 128, width), f32), pltpu.VMEM((16, 8, width), f32)]
        + turn_sems(2)
        + turn_sems(1)
        + [dma((2, 4))]
        + [dma((2, len(COLORS), 4)), dma((2, 2, len(COLORS), 4)), dma((2, 2, len(COLORS), 16))],
        compiler_params=pltpu.CompilerParams(collective_id=1, has_side_effects=True, vmem_limit_bytes=60 * 2**20),
        name="residual",
    )(
        amplitudes.reshape(pairs, rows, width),
        integrals.reshape(pairs, rows, width),
        fock_virtual,
        screening.reshape(screening.shape[2:]),
    )
    return out.reshape(shape)


def solution(mesh):
    placed = (
        P("oi", "oj", "vir", None),
        P("oi", "oj", "vir", None),
        P("vir", None),
        P("oi", "oj", None, None),
    )
    return jax.shard_map(
        body, mesh=mesh, in_specs=placed, out_specs=P("oi", "oj", "vir", None), check_vma=False
    )
```
